256 devices in a mesh: train: 16 (over y_lo, z), test: 16 (over x, y_hi, core).
Axes of the slice: x: 4, y: 4 (y_hi: 2, y_lo: 2; y = y_hi * 2 + y_lo), z: 8, core: 2. Of those that a mesh axis runs over, the one named last changes fastest.
Arguments:
- query_out: bfloat16 [4096, 3584], P('train', 'test'), may hold values from -16 to 16, as said below
- query_in: bfloat16 [4096, 3584], P('train', 'test'), may hold values from -6 to 6
- passage_out: bfloat16 [4096, 3584], P('train', 'test'), may hold values from -16 to 16, as said below
- passage_in_sum: bfloat16 [4096, 3584], P('train', 'test'), may hold values from -192 to 192
- passage_len: int32 [4096], P('train'), may hold values from 16 to 512
- positive: int32 [4096], P('train'), may hold values from 0 to 4095
- proj_in: bfloat16 [3584, 64], P('test'), may hold values from -0.09375 to 0.09375
- proj_out: bfloat16 [3584, 64], P('test'), may hold values from -0.09375 to 0.09375
- test_grads: bfloat16 [16384, 4096], P(('test', 'train')), may hold values from -6 to 6
Outputs:
- scores: float32 [4096, 16384], P('train', 'test')
The draws below stay inside these ranges and needn't reach their ends.
Inputs may be any that keep to these rules, and one draw needn't show every extreme that they name: `query_out`: entries stay within the range. `passage_out`: entries stay within the range.
All inputs are finite; a program needn't handle non-finite values.
Results may differ from the reference program's by a relative error of at most 0.0034.
Values may be sent and summed in bfloat16 or wider, within the bound.
A program may use at most 64 MiB of HBM per device.

```python
import math
import jax
import jax.numpy as jnp
from jax import lax

D = 3584
RANK = 64
PROJ = 4096
BATCH = 4096
NTEST = 16384


def draw_embeddings(key):
    keys = jax.random.split(jax.random.fold_in(key, 7), 6)
    queries = jax.random.normal(keys[0], (BATCH, D), jnp.float32)
    passages = jax.random.normal(keys[1], (BATCH, D), jnp.float32)
    chosen = jnp.arange(16, dtype=jnp.int32) * (BATCH // 16) + jax.random.randint(keys[4], (16,), 0, BATCH // 16)
    targets = (chosen + BATCH // 2) % BATCH
    second = (targets + 1) % BATCH
    target_logit = jnp.tile(jnp.array([120.0, 180.0, 240.0, 320.0], jnp.float32), 4)[:, None]
    strength = jnp.sqrt(target_logit) / float(D) ** 0.25
    shared = jnp.clip(jax.random.normal(keys[5], (16, D), jnp.float32), -2.5, 2.5) * strength
    queries = queries.at[chosen].set(shared)
    passages = passages.at[targets].set(shared)
    passages = passages.at[second].set(0.99 * shared)
    return (jnp.clip(queries, -16.0, 16.0), jnp.clip(passages, -16.0, 16.0))


def draw_query_out(key, part):
    return draw_embeddings(key)[0].astype(jnp.bfloat16)


def draw_passage_out(key, part):
    return draw_embeddings(key)[1].astype(jnp.bfloat16)


def with_ends(drawn, rng, smallest, high):
    shape = drawn.shape
    index_at = [jax.random.randint(jax.random.fold_in(rng, axis), (), 0, shape[axis]) for axis in range(len(shape))]
    drawn = drawn.at[tuple(index_at)].set(smallest)
    longest = shape.index(max(shape))
    index_at[longest] = (index_at[longest] + 1) % shape[longest]
    return drawn.at[tuple(index_at)].set(high)


def level_of(key, shape, pieces, least, high):
    gain, own = 1.0, jax.random.fold_in(key, 6)
    for axis_at, parts in pieces:
        steps = jnp.exp(jax.random.uniform(jax.random.fold_in(own, axis_at), (parts,), jnp.float32, least / len(pieces), high / len(pieces)))
        gain = gain * jnp.repeat(steps, shape[axis_at] // parts).reshape([-1 if axis == axis_at else 1 for axis in range(len(shape))])
    return gain


def gaussian(own_key, dims, spread, limit, pieces=(), kind=jnp.bfloat16):
    gain = level_of(own_key, dims, pieces, -0.22, 0.18) if pieces else 1.0
    values = jax.random.normal(own_key, dims, jnp.float32) * spread * gain
    return jnp.minimum(jnp.maximum(values, -limit), limit).astype(kind)


def setup_inputs(seed: int = 0) -> dict:
    key_of = jax.random.split(jax.random.key(seed), 10)
    query_out = draw_query_out(jax.random.fold_in(key_of[9], 71), 0)
    query_in = gaussian(key_of[1], (BATCH, D), 1.0, 6.0, ((0, 16), (1, 16)))
    passage_out = draw_passage_out(jax.random.fold_in(key_of[9], 71), 0)
    passage_in_sum = gaussian(key_of[3], (BATCH, D), 32.0, 192.0, ((0, 16), (1, 16)))
    passage_len = with_ends(jax.random.randint(key_of[4], (BATCH,), 16, 513), jax.random.fold_in(key_of[4], 1), 16, 512).astype(jnp.int32)
    positive = with_ends(jax.random.randint(key_of[5], (BATCH,), 0, BATCH), jax.random.fold_in(key_of[5], 1), 0, BATCH - 1).astype(jnp.int32)
    proj_in = gaussian(key_of[6], (D, RANK), D ** -0.5, 0.09375, ((0, 16),))
    proj_out = gaussian(key_of[7], (D, RANK), D ** -0.5, 0.09375, ((0, 16),))
    test_grads = gaussian(key_of[8], (NTEST, PROJ), 1.0, 6.0, ((0, 256),))
    return dict(query_out=query_out, query_in=query_in, passage_out=passage_out, passage_in_sum=passage_in_sum, passage_len=passage_len, positive=positive, proj_in=proj_in, proj_out=proj_out, test_grads=test_grads)


def reference(query_out, query_in, passage_out, passage_in_sum, passage_len, positive, proj_in, proj_out, test_grads):
    logit_scale = 1.0 / math.sqrt(D)
    logits = jnp.dot(query_out, passage_out.T, preferred_element_type=jnp.float32) * logit_scale
    row_top = lax.optimization_barrier(jnp.max(logits, axis=1, keepdims=True))
    exp_terms = jnp.exp(logits - row_top)
    prob = exp_terms / lax.optimization_barrier(jnp.sum(exp_terms, axis=1, keepdims=True))
    columns = jnp.arange(BATCH, dtype=jnp.int32)
    is_positive = (columns[None, :] == positive[:, None]).astype(jnp.float32)
    dlogit = (prob - is_positive).astype(jnp.bfloat16)
    grad_query = jnp.dot(dlogit, passage_out, preferred_element_type=jnp.float32) * logit_scale
    grad_pass = jnp.dot(dlogit.T, query_out, preferred_element_type=jnp.float32) * logit_scale
    proj_wide = proj_out.astype(jnp.float32)
    act_query = jnp.dot(query_in, proj_in, preferred_element_type=jnp.float32)
    act_pass = jnp.dot(passage_in_sum, proj_in, preferred_element_type=jnp.float32) / passage_len[:, None].astype(jnp.float32)
    out_query = jnp.dot(grad_query, proj_wide, precision=lax.Precision.HIGHEST)
    out_pass = jnp.dot(grad_pass, proj_wide, precision=lax.Precision.HIGHEST)
    train_grads = act_query[:, :, None] * out_query[:, None, :] + act_pass[:, :, None] * out_pass[:, None, :]
    train_grads = train_grads.reshape(BATCH, RANK * RANK).astype(jnp.bfloat16)
    return jnp.dot(train_grads, test_grads.T, preferred_element_type=jnp.float32)
```

```python
import math

import jax
import jax.numpy as jnp
from jax import lax
from jax.experimental import pallas as pl
from jax.experimental.pallas import tpu as pltpu
from jax.sharding import PartitionSpec as P

D = 3584
MESH = pl.DeviceIdType.MESH
F32, BF16 = jnp.float32, jnp.bfloat16

NAMES = {}


def sem_names():
    at = 0
    for name, count in (
        ("q1", 1), ("q10", 1), ("q2", 1), ("q3", 1), ("rq", 16),
        ("p", 1), ("p0", 1), ("rp", 1), ("pos", 1), ("rpos", 1),
        ("r1", 1), ("r10", 1), ("rr1", 1),
        ("pa", 4), ("pb", 3), ("ps", 1), ("rpa", 4), ("rpb", 3), ("rps", 1),
        ("lg", 1), ("ga", 4), ("gb", 3), ("rga", 4), ("rgb", 3),
        ("fa", 1), ("rfa", 1), ("qp", 1), ("rqp", 1), ("pp", 1), ("rpp", 1),
        ("st", 1), ("rst", 1), ("oq", 1), ("roq", 1), ("op", 1), ("rop", 1),
        ("fo", 1), ("rfo", 1), ("out", 2), ("rout", 2),
    ):
        NAMES[name] = at
        at += count
    return at


NSEM = sem_names()


def dev(x, y, z, c):
    return {"train": lax.rem(y, 2) * 8 + z, "test": x * 4 + lax.div(y, 2) * 2 + c}


def loop(first, last, body):
    def step(k, carry):
        body(k)
        return carry

    lax.fori_loop(first, last, step, 0)


def split(value):
    high = value.astype(BF16)
    return high, (value - high.astype(F32)).astype(BF16)


def kernel(
    q_ref, p_ref, qin_ref, pin_ref, len_ref, pos_ref, pjin_ref, pjout_ref, g_ref, out_ref,
    qj, pj, gb, r1s, r1r, fa, fo, qp2, pp2, st, oqs, oqr, ops, opr, posr, fat, fot, tt, outs, outr, sems,
):
    me_t, me_s = lax.axis_index("train"), lax.axis_index("test")
    b, z = lax.div(me_t, 8), lax.rem(me_t, 8)
    x, yh, c = lax.div(me_s, 4), lax.rem(lax.div(me_s, 2), 2), lax.rem(me_s, 2)
    y = yh * 2 + b
    q = x * 4 + y
    d = 1 - 2 * c
    scale = 1.0 / math.sqrt(D)

    def sem(name, k=0):
        return sems.at[NAMES[name] + k]

    def send(src, dst, ssem, rsem, to):
        pltpu.make_async_remote_copy(
            src_ref=src, dst_ref=dst, send_sem=ssem, recv_sem=rsem, device_id=to, device_id_type=MESH
        ).start()

    def wait(view, s):
        pltpu.make_async_copy(view, view, s).wait()

    def at_chip(k, core):
        q2 = lax.rem(q + k, 16)
        return q2, dev(lax.div(q2, 4), lax.rem(q2, 4), z, core)

    def near(src, dst, ssem, rsem):
        @pl.when(c == b)
        def _():
            pltpu.make_async_copy(src, dst, rsem).start()

        @pl.when(c != b)
        def _():
            send(src, dst, ssem, rsem, dev(x, y, z, b))

    barrier = pltpu.get_barrier_semaphore()

    def greet_plane(k):
        n = lax.rem(q * 2 + c + k, 32)
        q2 = lax.div(n, 2)
        pl.semaphore_signal(
            barrier, inc=1, device_id=dev(lax.div(q2, 4), lax.rem(q2, 4), z, lax.rem(n, 2)), device_id_type=MESH
        )

    def greet_ring(k):
        for core in range(2):
            pl.semaphore_signal(
                barrier, inc=1, device_id=dev(x, y, lax.rem(z + k, 8), core), device_id_type=MESH
            )

    loop(1, 32, greet_plane)
    loop(1, 8, greet_ring)
    pl.semaphore_wait(barrier, 45)

    slab = pl.ds(pl.multiple_of(z * 32 + b * 16, 16), 16)

    def send_p(k):
        q2, to = at_chip(k, b)
        send(p_ref.at[pl.ds(pl.multiple_of(q2 * 16, 16), 16)], pj.at[me_s, slab], sem("p"), sem("rp"), to)

    loop(1, 16, send_p)
    near(p_ref.at[pl.ds(pl.multiple_of(q * 16, 16), 16)], pj.at[me_s, slab], sem("p0"), sem("rp"))
    for k in (1, 3, 2):
        to = dev(lax.rem(x + k * c, 4), lax.rem(y + k * (1 - c), 4), z, b)
        send(q_ref, qj.at[me_s], sem("q1"), sem("rq", me_s), to)
    near(q_ref, qj.at[me_s], sem("q10"), sem("rq", me_s))
    send(pos_ref, posr, sem("pos"), sem("rpos"), dev(x, y + 1 - 2 * b, z, c))

    part = jnp.concatenate(
        [
            jnp.dot(pjin_ref[...], qin_ref[...], preferred_element_type=F32),
            jnp.dot(pjin_ref[...], pin_ref[...], preferred_element_type=F32) / len_ref[...].astype(F32),
            jnp.dot(pjout_ref[...], q_ref[...], preferred_element_type=F32),
            lax.dot_general(pjout_ref[...], p_ref[...], (((1,), (1,)), ((), ())), preferred_element_type=F32),
        ],
        axis=0,
    )
    r1s[...] = part.T.reshape(r1s.shape)

    def send_r1(k):
        q2, to = at_chip(k, b)
        send(r1s.at[q2], r1r.at[me_s], sem("r1"), sem("rr1"), to)

    loop(1, 16, send_r1)
    near(r1s.at[q], r1r.at[me_s], sem("r10"), sem("rr1"))

    to_a = dev(x, y, lax.rem(z + 8 + d, 8), c)
    to_b = dev(x, y, lax.rem(z + 8 - d, 8), c)
    to_sib = dev(x, y, z, 1 - c)

    def from_a(s):
        return lax.rem(z + 8 - d * s, 8)

    def from_b(s):
        return lax.rem(z + 8 + d * s, 8)

    def p_slab(zz):
        return pj.at[:, pl.ds(pl.multiple_of(zz * 32 + c * 16, 16), 16)]

    mine = p_slab(z)
    wait(mine, sem("rp"))
    send(mine, mine, sem("pa"), sem("rpa"), to_a)
    send(mine, mine, sem("pb"), sem("rpb"), to_b)
    send(mine, mine, sem("ps"), sem("rps"), to_sib)

    def start_g():
        pltpu.make_async_copy(g_ref, gb.at[z], sem("lg")).start()
        send(g_ref, gb.at[z], sem("ga"), sem("rga"), to_a)
        send(g_ref, gb.at[z], sem("gb"), sem("rgb"), to_b)

    def p_step(s):
        got = p_slab(from_a(s))
        wait(got, sem("rpa", s - 1))
        if s < 4:
            send(got, got, sem("pa", s), sem("rpa", s), to_a)
        send(got, got, sem("ps"), sem("rps"), to_sib)
        if s < 4:
            got = p_slab(from_b(s))
            wait(got, sem("rpb", s - 1))
            if s < 3:
                send(got, got, sem("pb", s), sem("rpb", s), to_b)
            send(got, got, sem("ps"), sem("rps"), to_sib)

    def g_step(s):
        got = gb.at[from_a(s)]
        wait(got, sem("rga", s - 1))
        if s < 4:
            send(got, got, sem("ga", s), sem("rga", s), to_a)
        if s < 4:
            got = gb.at[from_b(s)]
            wait(got, sem("rgb", s - 1))
            if s < 3:
                send(got, got, sem("gb", s), sem("rgb", s), to_b)

    start_g()

    for half in range(2):
        slot = x * 4 + half * 2
        wait(qj.at[slot], sem("rq", slot))
        for k in (1, 3, 2):
            send(qj.at[slot], qj.at[slot], sem("q2"), sem("rq", slot), dev(lax.rem(x + k, 4), y, z, c))

    @pl.when(c == b)
    def _():
        for x0 in range(4):
            slot = x0 * 4 + yh * 2 + 1
            wait(qj.at[slot], sem("rq", slot))
            for k in (1, 3, 2):
                send(qj.at[slot], qj.at[slot], sem("q3"), sem("rq", slot), dev(x, lax.rem(y + k, 4), z, c))

    p_step(1)

    wait(r1r, sem("rr1"))
    sums = jnp.sum(r1r[...], axis=0)
    row = c * 16 + q
    col = z * 2 + c
    fa[row] = sums[:, :128]
    qp2[q] = sums[:, 128:]
    pp2[col] = sums[:, 128:]

    def to_plane(buf, s, r):
        def body(k):
            n = lax.rem(q * 2 + c + k, 32)
            q2 = lax.div(n, 2)
            send(buf.at[row], buf.at[row], sem(s), sem(r), dev(lax.div(q2, 4), lax.rem(q2, 4), z, lax.rem(n, 2)))

        loop(1, 32, body)

    def to_column(src_of, dst, s, r):
        def body(k):
            n = lax.rem(col + k, 16)
            send(src_of(n), dst.at[col], sem(s), sem(r), dev(x, y, lax.div(n, 2), lax.rem(n, 2)))

        loop(1, 16, body)

    def to_chips(src_of, dst, s, r):
        def body(k):
            q2, to = at_chip(k, c)
            send(src_of(q2), dst.at[q], sem(s), sem(r), to)

        loop(1, 16, body)

    to_chips(lambda n: qp2.at[q], qp2, "qp", "rqp")
    to_column(lambda n: pp2.at[col], pp2, "pp", "rpp")
    to_plane(fa, "fa", "rfa")

    p_step(2)
    p_step(3)
    p_step(4)
    g_step(1)

    wait(pj.at[:, pl.ds(0, 128)], sem("rps"))
    for x0 in range(1, 4):
        for half in range(2):
            slot = lax.rem(x + x0, 4) * 4 + half * 2
            wait(qj.at[slot], sem("rq", slot))
    for x0 in range(4):
        for half in range(2):

            @pl.when(jnp.logical_or(c != b, yh != half))
            def _():
                slot = x0 * 4 + half * 2 + 1
                wait(qj.at[slot], sem("rq", slot))

    logits = jnp.dot(pj[0], qj[0], preferred_element_type=F32)
    for j in range(1, 16):
        logits += jnp.dot(pj[j], qj[j], preferred_element_type=F32)
    logits *= scale
    top = jnp.max(logits, axis=0, keepdims=True)
    total = jnp.sum(jnp.exp(logits - top), axis=0, keepdims=True)
    st[q, 0:1] = top
    st[q, 1:2] = total
    to_chips(lambda n: st.at[q], st, "st", "rst")
    wait(posr, sem("rpos"))
    positive = jnp.where(c == b, pos_ref[...], posr[...])
    at = lax.broadcasted_iota(jnp.int32, logits.shape, 0)
    passage = (((at >> 4) & 1) * 8 + (at >> 5)) * 256 + q * 16 + (at & 15)
    hit = (passage == positive).astype(F32)
    wait(qp2.at[pl.ds(0, 15)], sem("rqp"))
    wait(pp2.at[pl.ds(0, 15)], sem("rpp"))
    qp_high, qp_low = split(qp2[...].reshape(256, 128))
    pp_high, pp_low = split(pp2[...].reshape(256, 128).T)
    g_step(2)
    wait(st.at[pl.ds(0, 15)], sem("rst"))
    tops, totals = st[:, 0, :], st[:, 1, :]
    row_top = jnp.max(tops, axis=0, keepdims=True)
    row_sum = jnp.sum(totals * jnp.exp(tops - row_top), axis=0, keepdims=True)
    dlogit = (jnp.exp(logits - row_top) / row_sum - hit).astype(BF16)
    oq = jnp.dot(pp_high, dlogit, preferred_element_type=F32) + jnp.dot(pp_low, dlogit, preferred_element_type=F32)
    oqs[...] = (oq * scale).T.reshape(oqs.shape)
    to_chips(lambda n: oqs.at[n], oqr, "oq", "roq")
    op = jnp.dot(dlogit, qp_high, preferred_element_type=F32) + jnp.dot(dlogit, qp_low, preferred_element_type=F32)
    ops[...] = (op * scale).reshape(ops.shape)
    to_column(lambda n: ops.at[n], opr, "op", "rop")
    oqr[q] = oqs[q]
    opr[col] = ops[col]
    wait(fa.at[pl.ds(0, 31)], sem("rfa"))
    for i in range(2):
        fat[i] = fa[i * 16 : i * 16 + 16].reshape(256, 128).T
    wait(oqr.at[pl.ds(0, 15)], sem("roq"))
    wait(opr.at[pl.ds(0, 15)], sem("rop"))
    lane = lax.broadcasted_iota(jnp.int32, (16, 128), 1)
    fo[row] = jnp.where(lane < 64, jnp.sum(opr[...], axis=0), jnp.sum(oqr[...], axis=0))
    to_plane(fo, "fo", "rfo")
    g_step(3)
    wait(fo.at[pl.ds(0, 31)], sem("rfo"))
    for i in range(2):
        fot[i] = fo[i * 16 : i * 16 + 16].reshape(256, 128).T

    def build(block):
        op_t, oq_t = fot[block, 0:64], fot[block, 64:128]

        def body(r, carry):
            aq = fat[block, pl.ds(r, 1)]
            ap = fat[block, pl.ds(64 + r, 1)]
            tt[pl.ds(pl.multiple_of(r * 64, 64), 64)] = (aq * oq_t + ap * op_t).astype(BF16)
            return carry

        lax.fori_loop(0, 64, body, 0, unroll=4)

    build(1 - b)
    wait(g_ref, sem("lg"))
    g_step(4)
    partner = dev(x, y + 1 - 2 * b, z, c)
    for h in range(2):
        half = gb[h * 4 : h * 4 + 4].reshape(256, 4096)
        outs[h] = jnp.dot(half, tt[...], preferred_element_type=F32).astype(BF16)
        send(outs.at[h], outr.at[h], sem("out", h), sem("rout", h), partner)
    build(b)
    for h in range(2):
        half = gb[h * 4 : h * 4 + 4].reshape(256, 4096)
        out_ref[b, h * 256 : h * 256 + 256] = jnp.dot(half, tt[...], preferred_element_type=F32)

    wait(p_ref.at[pl.ds(0, 240)], sem("p"))
    wait(qj.at[pl.ds(0, 3)], sem("q1"))
    wait(r1s.at[pl.ds(0, 15)], sem("r1"))
    wait(pos_ref, sem("pos"))
    wait(qj.at[pl.ds(0, 6)], sem("q2"))

    @pl.when(c == b)
    def _():
        wait(qj.at[pl.ds(0, 12)], sem("q3"))

    @pl.when(c != b)
    def _():
        wait(p_ref.at[pl.ds(0, 16)], sem("p0"))
        wait(qj.at[0], sem("q10"))
        wait(r1s.at[0], sem("r10"))

    for s in range(4):
        wait(mine, sem("pa", s))
        wait(g_ref, sem("ga", s))
    for s in range(3):
        wait(mine, sem("pb", s))
        wait(g_ref, sem("gb", s))
    wait(pj.at[:, pl.ds(0, 128)], sem("ps"))
    wait(qp2.at[pl.ds(0, 15)], sem("qp"))
    wait(pp2.at[pl.ds(0, 15)], sem("pp"))
    wait(fa.at[pl.ds(0, 31)], sem("fa"))
    wait(st.at[pl.ds(0, 15)], sem("st"))
    wait(oqs.at[pl.ds(0, 15)], sem("oq"))
    wait(ops.at[pl.ds(0, 15)], sem("op"))
    wait(fo.at[pl.ds(0, 31)], sem("fo"))
    for h in range(2):
        wait(outr.at[h], sem("rout", h))
        out_ref[1 - b, h * 256 : h * 256 + 256] = outr[h].astype(F32)
        wait(outs.at[h], sem("out", h))


def local(
    query_out, query_in, passage_out, passage_in_sum, passage_len, positive, proj_in, proj_out, test_grads
):
    vmem = pl.BlockSpec(memory_space=pltpu.VMEM)
    out = pl.pallas_call(
        kernel,
        name="attribution",
        out_shape=jax.ShapeDtypeStruct((2, 512, 256), F32),
        in_specs=[vmem] * 8 + [pl.BlockSpec(memory_space=pl.ANY)],
        out_specs=vmem,
        scratch_shapes=[
            pltpu.VMEM((16, 224, 256), BF16),
            pltpu.VMEM((16, 256, 224), BF16),
            pltpu.VMEM((8, 64, 4096), BF16),
            pltpu.VMEM((16, 16, 256), F32),
            pltpu.VMEM((16, 16, 256), F32),
            pltpu.VMEM((32, 16, 128), F32),
            pltpu.VMEM((32, 16, 128), F32),
            pltpu.VMEM((16, 16, 128), F32),
            pltpu.VMEM((16, 16, 128), F32),
            pltpu.VMEM((16, 2, 256), F32),
            pltpu.VMEM((16, 16, 128), F32),
            pltpu.VMEM((16, 16, 128), F32),
            pltpu.VMEM((16, 16, 128), F32),
            pltpu.VMEM((16, 16, 128), F32),
            pltpu.VMEM((1, 256), jnp.int32),
            pltpu.VMEM((2, 128, 256), F32),
            pltpu.VMEM((2, 128, 256), F32),
            pltpu.VMEM((4096, 256), BF16),
            pltpu.VMEM((2, 256, 256), BF16),
            pltpu.VMEM((2, 256, 256), BF16),
            pltpu.SemaphoreType.DMA((NSEM,)),
        ],
        compiler_params=pltpu.CompilerParams(
            collective_id=0, has_side_effects=True, vmem_limit_bytes=48 * 1024 * 1024
        ),
    )(
        query_out.T,
        passage_out,
        query_in.T,
        passage_in_sum.T,
        passage_len[None, :],
        positive[None, :],
        proj_in.T,
        proj_out.T,
        test_grads,
    )
    return out.reshape(1024, 256).T


def solution(mesh):
    return jax.shard_map(
        local,
        mesh=mesh,
        in_specs=(
            P("train", "test"),
            P("train", "test"),
            P("train", "test"),
            P("train", "test"),
            P("train"),
            P("train"),
            P("test", None),
            P("test", None),
            P(("test", "train"), None),
        ),
        out_specs=P("train", "test"),
        check_vma=False,
    )
```

```python
import math

import jax
import jax.numpy as jnp
from jax import lax
from jax.experimental import pallas as pl
from jax.experimental.pallas import tpu as pltpu
from jax.sharding import PartitionSpec as P

D = 3584
MESH = pl.DeviceIdType.MESH
F32, BF16 = jnp.float32, jnp.bfloat16

NAMES = {}


def sem_names():
    at = 0
    for name, count in (
        ("in", 8), ("q1", 1), ("q10", 1), ("q2", 1), ("rq", 16),
        ("p", 1), ("p0", 1), ("rp", 1), ("pos", 1), ("rpos", 1),
        ("r1", 1), ("r10", 1), ("rr1", 1),
        ("pa", 1), ("pb", 1), ("ps", 1), ("rpa", 4), ("rpb", 3), ("rps", 1),
        ("lg", 1), ("ga", 1), ("gb", 1), ("rga", 16), ("rgb", 12),
        ("fa", 1), ("rfa", 1),
        ("st", 1), ("rst", 1), ("oq", 1), ("roq", 1), ("op", 1), ("rop", 1),
        ("fo", 1), ("rfo", 1), ("out", 2), ("rout", 2),
    ):
        NAMES[name] = at
        at += count
    return at


NSEM = sem_names()


def dev(x, y, z, c):
    return {"train": lax.rem(y, 2) * 8 + z, "test": x * 4 + lax.div(y, 2) * 2 + c}


def loop(first, last, body):
    def step(k, carry):
        body(k)
        return carry

    lax.fori_loop(first, last, step, 0)


def split(value):
    high = value.astype(BF16)
    return high, (value - high.astype(F32)).astype(BF16)


def dot(a, b, dims=((1,), (0,))):
    return lax.dot_general(a, b, (dims, ((), ())), preferred_element_type=F32)


def kernel(
    q_hbm, p_hbm, qin_hbm, pin_hbm, len_hbm, pos_hbm, pjin_hbm, pjout_hbm, g_ref, out_ref,
    qx, pt, pr, qin, pin, plen, posv, pjin, pjout,
    qj, pj, gb, r1s, r1r, fa, fo, st, oqs, oqr, ops, opr, posr, fat, fot, tt, outs, outr, sems,
):
    me_t, me_s = lax.axis_index("train"), lax.axis_index("test")
    b, z = lax.div(me_t, 8), lax.rem(me_t, 8)
    x, yh, c = lax.div(me_s, 4), lax.rem(lax.div(me_s, 2), 2), lax.rem(me_s, 2)
    y = yh * 2 + b
    q = x * 4 + y
    d = 1 - 2 * c
    row = c * 16 + q
    col = z * 2 + c
    scale = 1.0 / math.sqrt(D)

    def sem(name, k=0):
        return sems.at[NAMES[name] + k]

    def send(src, dst, ssem, rsem, to):
        pltpu.make_async_remote_copy(
            src_ref=src, dst_ref=dst, send_sem=ssem, recv_sem=rsem, device_id=to, device_id_type=MESH
        ).start()

    def wait(view, s):
        pltpu.make_async_copy(view, view, s).wait()

    def at_chip(k, core):
        q2 = lax.rem(q + k, 16)
        return q2, dev(lax.div(q2, 4), lax.rem(q2, 4), z, core)

    def beside(dx, dy, core):
        return dev(lax.rem(x + 4 + dx, 4), lax.rem(y + 4 + dy, 4), z, core)

    def near(src, dst, ssem, rsem):
        @pl.when(c == b)
        def _():
            pltpu.make_async_copy(src, dst, rsem).start()

        @pl.when(c != b)
        def _():
            send(src, dst, ssem, rsem, dev(x, y, z, b))

    loads = ((q_hbm, qx.at[0:224]), (p_hbm, pt), (qin_hbm, qin), (pin_hbm, pin), (len_hbm, plen), (pos_hbm, posv), (pjin_hbm, pjin), (pjout_hbm, pjout))
    loads = [pltpu.make_async_copy(a, v, sem("in", i)) for i, (a, v) in enumerate(loads)]
    for i in (1, 0, 7, 2, 3, 4, 6, 5):
        loads[i].start()
    pltpu.make_async_copy(g_ref, gb.at[0], sem("lg")).start()
    barrier = pltpu.get_barrier_semaphore()

    def greet_plane(k):
        n = lax.rem(q * 2 + c + k, 32)
        q2 = lax.div(n, 2)
        pl.semaphore_signal(
            barrier, inc=1, device_id=dev(lax.div(q2, 4), lax.rem(q2, 4), z, lax.rem(n, 2)), device_id_type=MESH
        )

    def greet_ring(k):
        for core in range(2):
            pl.semaphore_signal(
                barrier, inc=1, device_id=dev(x, y, lax.rem(z + k, 8), core), device_id_type=MESH
            )

    loop(1, 8, greet_ring)
    loop(1, 32, greet_plane)
    loads[1].wait()
    pr[...] = pt[...].T
    loads[7].wait()
    qx[224:288, 128:256] = jnp.zeros((64, 128), BF16)
    qx[224:288, 0:224] = pjout[...]
    for i in (0, 2, 3, 4, 6, 5):
        loads[i].wait()
    part = jnp.concatenate([dot(pjin[...], qin[...]), dot(pjin[...], pin[...]) / plen[...].astype(F32)], axis=0)
    r1s[...] = part.T.reshape(r1s.shape)
    pl.semaphore_wait(barrier, 45)

    slab = pl.ds(pl.multiple_of(z * 32 + b * 16, 16), 16)

    def send_p(k):
        q2, to = at_chip(k, b)
        send(pr.at[pl.ds(pl.multiple_of(q2 * 16, 16), 16)], pj.at[me_s, slab], sem("p"), sem("rp"), to)

    loop(1, 16, send_p)
    near(pr.at[pl.ds(pl.multiple_of(q * 16, 16), 16)], pj.at[me_s, slab], sem("p0"), sem("rp"))
    near(qx, qj.at[me_s], sem("q10"), sem("rq", me_s))
    for k in (1, -1):
        send(qx, qj.at[me_s], sem("q1"), sem("rq", me_s), beside(k * c, k * (1 - c), b))
    send(posv, posr, sem("pos"), sem("rpos"), dev(x, y + 1 - 2 * b, z, c))

    to_a = dev(x, y, lax.rem(z + 8 + d, 8), c)
    to_b = dev(x, y, lax.rem(z + 8 - d, 8), c)
    to_sib = dev(x, y, z, 1 - c)

    def from_a(s):
        return lax.rem(z + 8 - d * s, 8)

    def from_b(s):
        return lax.rem(z + 8 + d * s, 8)

    def p_slab(zz):
        return pj.at[:, pl.ds(pl.multiple_of(zz * 32 + c * 16, 16), 16)]

    def p_step(s):
        got = p_slab(from_a(s))
        wait(got, sem("rpa", s - 1))
        if s < 4:
            send(got, got, sem("pa"), sem("rpa", s), to_a)
        send(got, got, sem("ps"), sem("rps"), to_sib)
        if s < 4:
            got = p_slab(from_b(s))
            wait(got, sem("rpb", s - 1))
            if s < 3:
                send(got, got, sem("pb"), sem("rpb", s), to_b)
            send(got, got, sem("ps"), sem("rps"), to_sib)

    def g_event(e):
        s, rows = e // 4 + 1, slice(e % 4 * 16, e % 4 * 16 + 16)
        if e < 16:
            src = g_ref.at[rows]
            if s > 1:
                src = gb.at[2 * s - 3, rows]
                wait(src, sem("rga", e - 4))
            send(src, gb.at[2 * s - 1, rows], sem("ga"), sem("rga", e), to_a)
        if e < 12:
            src = g_ref.at[rows]
            if s > 1:
                src = gb.at[2 * s - 2, rows]
                wait(src, sem("rgb", e - 4))
            send(src, gb.at[2 * s, rows], sem("gb"), sem("rgb", e), to_b)

    g_event(0)
    g_event(1)

    def send_r1(k):
        q2, to = at_chip(k, b)
        send(r1s.at[q2], r1r.at[me_s], sem("r1"), sem("rr1"), to)

    loop(1, 16, send_r1)
    near(r1s.at[q], r1r.at[me_s], sem("r10"), sem("rr1"))

    HALVES = (slice(0, 144), slice(144, 288))

    def got_q(x0, half, core):
        slot = x0 * 4 + half * 2 + core
        wait(qj.at[slot], sem("rq", slot))
        return slot

    def pass_q(slot, dx, dy):
        send(qj.at[slot], qj.at[slot], sem("q2"), sem("rq", slot), beside(dx, dy, c))

    def pass_half(slot, h, dx, dy):
        view = qj.at[slot, HALVES[h]]
        send(view, view, sem("q2"), sem("rq", slot), beside(dx, dy, c))

    below, above = lax.div(lax.rem(y + 3, 4), 2), lax.div(lax.rem(y + 1, 4), 2)

    @pl.when(c == b)
    def _():
        slot = got_q(x, yh, 0)
        pass_q(slot, 1, 0)
        pass_q(slot, -1, 0)
        slot = got_q(x, yh, 1)
        pass_q(slot, 0, 1)
        pass_q(slot, 0, -1)

    mine = p_slab(z)
    wait(mine, sem("rp"))
    send(mine, mine, sem("pa"), sem("rpa"), to_a)
    send(mine, mine, sem("pb"), sem("rpb"), to_b)
    send(mine, mine, sem("ps"), sem("rps"), to_sib)

    @pl.when(c == b)
    def _():
        for h, dx in ((0, 1), (1, -1)):
            slot = got_q(lax.rem(x + 4 - dx, 4), yh, 1)
            pass_half(slot, h, dx, 0)
            pass_q(slot, 0, 1)
            pass_q(slot, 0, -1)

    @pl.when(c != b)
    def _():
        for h, dy, half in ((0, 1, below), (1, -1, above)):
            slot = got_q(x, half, 0)
            pass_half(slot, h, 0, dy)
            pass_q(slot, 1, 0)
            pass_q(slot, -1, 0)

    p_step(1)
    g_event(2)

    @pl.when(c == b)
    def _():
        slot = got_q(x, 1 - yh, 0)
        pass_q(slot, 1, 0)
        pass_q(slot, -1, 0)
        slot = got_q(lax.rem(x + 2, 4), yh, 1)
        pass_q(slot, 0, 1)
        pass_q(slot, 0, -1)

    @pl.when(c != b)
    def _():
        for x0 in (0, 1, 3):
            for h, dy, half in ((0, 1, below), (1, -1, above)):
                pass_half(got_q(lax.rem(x + x0, 4), half, 1), h, 0, dy)

    for h, dx in ((0, 1), (1, -1)):
        for half in range(2):
            pass_half(got_q(lax.rem(x + 4 - dx, 4), half, 0), h, dx, 0)

    p_step(2)
    g_event(3)

    @pl.when(c != b)
    def _():
        for h, dy, half in ((0, 1, below), (1, -1, above)):
            pass_half(got_q(lax.rem(x + 2, 4), half, 1), h, 0, dy)

    wait(r1r, sem("rr1"))
    fa[row] = jnp.sum(r1r[...], axis=0)
    p_step(3)
    g_event(4)
    p_step(4)
    g_event(5)

    def to_plane(buf, s, r):
        def body(k):
            n = lax.rem(q * 2 + c + k, 32)
            q2 = lax.div(n, 2)
            send(buf.at[row], buf.at[row], sem(s), sem(r), dev(lax.div(q2, 4), lax.rem(q2, 4), z, lax.rem(n, 2)))

        loop(1, 32, body)

    def to_column(src_of, dst, s, r):
        def body(k):
            n = lax.rem(col + k, 16)
            send(src_of(n), dst.at[col], sem(s), sem(r), dev(x, y, lax.div(n, 2), lax.rem(n, 2)))

        loop(1, 16, body)

    def to_chips(src_of, dst, s, r):
        def body(k):
            q2, to = at_chip(k, c)
            send(src_of(q2), dst.at[q], sem(s), sem(r), to)

        loop(1, 16, body)

    for half in range(2):
        got_q(lax.rem(x + 2, 4), half, 0)

    @pl.when(c == b)
    def _():
        for x0 in range(4):
            got_q(x0, 1 - yh, 1)

    wait(pj.at[:, pl.ds(0, 128)], sem("rps"))
    logits = dot(pj[0], qj[0, 0:224])
    for j in range(1, 16):
        logits += dot(pj[j], qj[j, 0:224])
    logits *= scale
    top = jnp.max(logits, axis=0, keepdims=True)
    total = jnp.sum(jnp.exp(logits - top), axis=0, keepdims=True)
    st[q, 0:1] = top
    st[q, 1:2] = total
    to_chips(lambda n: st.at[q], st, "st", "rst")
    to_plane(fa, "fa", "rfa")
    g_event(6)
    wait(posr, sem("rpos"))
    positive = jnp.where(c == b, posv[...], posr[...])
    at = lax.broadcasted_iota(jnp.int32, logits.shape, 0)
    passage = (((at >> 4) & 1) * 8 + (at >> 5)) * 256 + q * 16 + (at & 15)
    hit = (passage == positive).astype(F32)
    qp_t = dot(qj[0, 224:288, 0:224], qj[0, 0:224])
    pp_t = dot(qj[0, 224:288, 0:224], pj[0], ((1,), (1,)))
    for j in range(1, 16):
        qp_t += dot(qj[j, 224:288, 0:224], qj[j, 0:224])
        pp_t += dot(qj[j, 224:288, 0:224], pj[j], ((1,), (1,)))
    qp_high, qp_low = split(qp_t)
    pp_high, pp_low = split(pp_t)
    wait(st.at[pl.ds(0, 15)], sem("rst"))
    tops, totals = st[:, 0, :], st[:, 1, :]
    row_top = jnp.max(tops, axis=0, keepdims=True)
    row_sum = jnp.sum(totals * jnp.exp(tops - row_top), axis=0, keepdims=True)
    dlogit = (jnp.exp(logits - row_top) / row_sum - hit).astype(BF16)
    op = dot(dlogit, qp_high, ((1,), (1,))) + dot(dlogit, qp_low, ((1,), (1,)))
    ops[...] = (op * scale).reshape(ops.shape)
    to_column(lambda n: ops.at[n], opr, "op", "rop")
    oq = dot(pp_high, dlogit) + dot(pp_low, dlogit)
    oqs[...] = (oq * scale).T.reshape(oqs.shape)
    to_chips(lambda n: oqs.at[n], oqr, "oq", "roq")
    oqr[q] = oqs[q]
    opr[col] = ops[col]
    g_event(7)
    g_event(8)
    wait(fa.at[pl.ds(0, 31)], sem("rfa"))
    for i in range(2):
        fat[i] = fa[i * 16 : i * 16 + 16].reshape(256, 128).T
    wait(oqr.at[pl.ds(0, 15)], sem("roq"))
    wait(opr.at[pl.ds(0, 15)], sem("rop"))
    fo[row] = jnp.concatenate([jnp.sum(opr[...], axis=0), jnp.sum(oqr[...], axis=0)], axis=1)
    to_plane(fo, "fo", "rfo")
    g_event(9)
    g_event(10)
    g_event(11)
    wait(fo.at[pl.ds(0, 31)], sem("rfo"))
    for i in range(2):
        fot[i] = fo[i * 16 : i * 16 + 16].reshape(256, 128).T

    def build(n, block):
        op_t, oq_t = fot[block, 0:64], fot[block, 64:128]

        def body(r, carry):
            aq = fat[block, pl.ds(r, 1)]
            ap = fat[block, pl.ds(64 + r, 1)]
            tt[n, pl.ds(pl.multiple_of(r * 64, 64), 64)] = (aq * oq_t + ap * op_t).astype(BF16)
            return carry

        lax.fori_loop(0, 64, body, 0, unroll=4)

    def place(slot):
        if slot == 0:
            at = z
        elif slot % 2:
            at = from_a((slot + 1) // 2)
        else:
            at = from_b(slot // 2)
        return pl.ds(pl.multiple_of(at * 64, 64), 64)

    partner = dev(x, y + 1 - 2 * b, z, c)

    def product(n, h):
        return dot(gb[h * 4 : h * 4 + 4].reshape(256, 4096), tt[n])

    def swap(h):
        outs[h] = product(0, h).astype(BF16)
        send(outs.at[h], outr.at[h], sem("out", h), sem("rout", h), partner)

    def keep(h):
        mine = product(1, h)
        for i in range(4):
            out_ref[b, place(h * 4 + i)] = mine[i * 64 : i * 64 + 64]

    build(0, 1 - b)
    g_event(12)
    g_event(13)
    wait(gb.at[0], sem("lg"))
    swap(0)
    g_event(14)
    build(1, b)
    keep(0)
    g_event(15)
    for e in range(12, 16):
        wait(gb.at[7, e % 4 * 16 : e % 4 * 16 + 16], sem("rga", e))
    for e in range(8, 12):
        wait(gb.at[6, e % 4 * 16 : e % 4 * 16 + 16], sem("rgb", e))
    swap(1)
    keep(1)

    wait(pr.at[pl.ds(0, 240)], sem("p"))
    wait(qj.at[pl.ds(0, 2)], sem("q1"))
    wait(r1s.at[pl.ds(0, 15)], sem("r1"))
    wait(posv, sem("pos"))

    @pl.when(c == b)
    def _():
        wait(qj.at[pl.ds(0, 15)], sem("q2"))

    @pl.when(c != b)
    def _():
        wait(qj.at[pl.ds(0, 11)], sem("q2"))
        wait(pr.at[pl.ds(0, 16)], sem("p0"))
        wait(qj.at[0], sem("q10"))
        wait(r1s.at[0], sem("r10"))

    wait(pj.at[:, pl.ds(0, 64)], sem("pa"))
    wait(pj.at[:, pl.ds(0, 48)], sem("pb"))
    wait(pj.at[:, pl.ds(0, 128)], sem("ps"))
    wait(gb.at[pl.ds(0, 4)], sem("ga"))
    wait(gb.at[pl.ds(0, 3)], sem("gb"))
    wait(fa.at[pl.ds(0, 31)], sem("fa"))
    wait(st.at[pl.ds(0, 15)], sem("st"))
    wait(oqs.at[pl.ds(0, 15)], sem("oq"))
    wait(ops.at[pl.ds(0, 15)], sem("op"))
    wait(fo.at[pl.ds(0, 31)], sem("fo"))
    for h in range(2):
        wait(outr.at[h], sem("rout", h))
        for i in range(4):
            out_ref[1 - b, place(h * 4 + i)] = outr[h, i * 64 : i * 64 + 64].astype(F32)
        wait(outs.at[h], sem("out", h))


def local(
    query_out, query_in, passage_out, passage_in_sum, passage_len, positive, proj_in, proj_out, test_grads
):
    out = pl.pallas_call(
        kernel,
        name="attribution",
        out_shape=jax.ShapeDtypeStruct((2, 512, 256), F32),
        in_specs=[pl.BlockSpec(memory_space=pl.ANY)] * 9,
        out_specs=pl.BlockSpec(memory_space=pltpu.VMEM),
        scratch_shapes=[
            pltpu.VMEM((288, 256), BF16),
            pltpu.VMEM((224, 256), BF16),
            pltpu.VMEM((256, 224), BF16),
            pltpu.VMEM((224, 256), BF16),
            pltpu.VMEM((224, 256), BF16),
            pltpu.VMEM((1, 256), jnp.int32),
            pltpu.VMEM((1, 256), jnp.int32),
            pltpu.VMEM((64, 224), BF16),
            pltpu.VMEM((64, 224), BF16),
            pltpu.VMEM((16, 288, 256), BF16),
            pltpu.VMEM((16, 256, 224), BF16),
            pltpu.VMEM((8, 64, 4096), BF16),
            pltpu.VMEM((16, 16, 128), F32),
            pltpu.VMEM((16, 16, 128), F32),
            pltpu.VMEM((32, 16, 128), F32),
            pltpu.VMEM((32, 16, 128), F32),
            pltpu.VMEM((16, 2, 256), F32),
            pltpu.VMEM((16, 16, 64), F32),
            pltpu.VMEM((16, 16, 64), F32),
            pltpu.VMEM((16, 16, 64), F32),
            pltpu.VMEM((16, 16, 64), F32),
            pltpu.VMEM((1, 256), jnp.int32),
            pltpu.VMEM((2, 128, 256), F32),
            pltpu.VMEM((2, 128, 256), F32),
            pltpu.VMEM((2, 4096, 256), BF16),
            pltpu.VMEM((2, 256, 256), BF16),
            pltpu.VMEM((2, 256, 256), BF16),
            pltpu.SemaphoreType.DMA((NSEM,)),
        ],
        compiler_params=pltpu.CompilerParams(
            collective_id=0, has_side_effects=True, vmem_limit_bytes=62 * 1024 * 1024
        ),
    )(
        query_out.T,
        passage_out.T,
        query_in.T,
        passage_in_sum.T,
        passage_len[None, :],
        positive[None, :],
        proj_in.T,
        proj_out.T,
        test_grads,
    )
    return out.reshape(1024, 256).T


def solution(mesh):
    return jax.shard_map(
        local,
        mesh=mesh,
        in_specs=(
            P("train", "test"),
            P("train", "test"),
            P("train", "test"),
            P("train", "test"),
            P("train"),
            P("train"),
            P("test", None),
            P("test", None),
            P(("test", "train"), None),
        ),
        out_specs=P("train", "test"),
        check_vma=False,
    )
```
